256 devices in a mesh: blk: 32 (over x, y, core), tok: 8 (over z).
Axes of the slice: x: 4, y: 4, z: 8, core: 2. Of those that a mesh axis runs over, the one named last changes fastest.
Arguments:
- hidden_in: bfloat16 [2, 6144, 1792], P(None, 'tok', 'blk'), may hold values from -6 to 6
- norm_gains: float32 [2, 2, 1792], replicated, may hold values from 0.25 to 1.75
- w_qk: bfloat16 [2, 1792, 512], P(None, 'blk'), may hold values from -0.125 to 0.125
- w_v: bfloat16 [2, 1792, 1792], P(None, None, 'blk'), may hold values from -0.125 to 0.125
- w_o: bfloat16 [2, 1792, 1792], P(None, 'blk'), may hold values from -0.25 to 0.25
- lm_head: bfloat16 [2, 28672, 1792], P(None, 'blk')
- state_pool: float32 [128, 2, 273, 1792], P('tok', None, None, 'blk')
- norm_pool: float32 [128, 2, 16, 273], P('tok')
- seq_lens: int32 [8, 8], P('tok'), may hold values from 1 to 384, 768 in all within a row
- page_slot: int32 [8, 8], P('tok'), may hold values from 0 to 15, as said below
- fresh: int32 [8, 8], P('tok'), may hold values 0 or 1
- targets: int32 [6144], P('tok'), may hold values from 0 to 28671
- owner_slot: int32 [64], P('tok'), may hold values from 0 to 63, each once
Outputs:
- token_logp: float32 [2, 6144], P(None, 'tok')
- seq_diffs: float32 [64], P('tok')
The draws below stay inside these ranges and needn't reach their ends.
Inputs may be any that keep to these rules, and one draw needn't show every extreme that they name: `page_slot`: in each row the 8 slots are distinct. `seq_lens`: each row sums to 768. `owner_slot`: every position is named once.
All inputs are finite; a program needn't handle non-finite values. No bound on the sum of `fresh` on one device may be relied on, other than what follows from the above.
Results may differ from the reference program's by a relative error of at most 0.025.
Values may be sent and summed in bfloat16 or wider, within the bound.
No kernel may reach another device: no remote copies, remote signals or barrier semaphores. Data moves between devices by JAX's collectives and lax.ppermute only.
A program may use at most 128 MiB of HBM per device.

```python
import math
import jax
import jax.numpy as jnp
import numpy as np
from jax import lax

D = 1792
HEADS = 16
FEAT_IN = 16
TOK_DEV = 768
SEQ_DEV = 8
POOL = 16
FEAT = 273
VOCAB = 28672
MOST_LEN = 384
TOKENS = 6144
SEQS = 64
N_TOK = 8


def taylor_feats_drawn(vector):
    lead = vector.shape[:-1]
    inner = vector.shape[-1]
    outer = vector[..., :, None] * vector[..., None, :]
    ones = jnp.ones_like(vector[..., :1])
    return jnp.concatenate([ones, vector, outer.reshape(lead + (inner * inner,)) * 0.5 ** 0.5], axis=-1)


def pool_parts(key):
    base = jax.random.fold_in(key, 71)
    prefix = jnp.exp(jax.random.uniform(jax.random.fold_in(base, 1), (N_TOK * POOL, 2, HEADS), minval=math.log(8.0), maxval=math.log(256.0)))
    first = jax.random.normal(jax.random.fold_in(base, 2), (N_TOK * POOL, 2, HEADS, FEAT_IN)) * 0.5
    second = jax.random.normal(jax.random.fold_in(base, 3), (N_TOK * POOL, 2, HEADS, FEAT_IN)) * 0.5
    return (prefix, first, second)


def draw_norm_pool(key, part):
    prefix, first, second = pool_parts(key)
    mixed = 0.5 * (taylor_feats_drawn(first) + taylor_feats_drawn(second))
    return (prefix[..., None] * mixed).astype(jnp.float32)


def draw_state_pool(key, part):
    prefix, first, second = pool_parts(key)
    columns = jnp.repeat(prefix, D // HEADS, axis=-1)
    shape = (N_TOK * POOL, 2, FEAT, D)
    noise = jax.random.normal(jax.random.fold_in(key, 5), shape)
    return (columns[:, :, None, :] * 0.4 * noise).astype(jnp.float32)


def draw_lm_head(key, part):
    spread = 3.0 / math.sqrt(D)
    base = jax.random.normal(jax.random.fold_in(key, 1), (2, VOCAB, D)) * spread
    return base.astype(jnp.bfloat16)


def draw_page_slot(key, part):

    def one_row(row_key):
        inner = jax.random.permutation(row_key, POOL - 2)[:SEQ_DEV - 2] + 1
        fixed_ends = jnp.array([0, POOL - 1], dtype=jnp.int32)
        joined = jnp.concatenate([fixed_ends, inner.astype(jnp.int32)])
        return jax.random.permutation(jax.random.fold_in(row_key, 9), joined)
    row_keys = jax.random.split(key, N_TOK)
    return jax.vmap(one_row)(row_keys).astype(jnp.int32)


def plant(values, stream_key, low, largest):
    longest = values.shape.index(max(values.shape))
    spots = []
    for shift in (0, 1):
        where = [jax.random.randint(jax.random.fold_in(stream_key, axis), (), 0, length) for axis, length in enumerate(values.shape)]
        where[longest] = (where[longest] + shift) % values.shape[longest]
        spots.append(tuple(where))
    return values.at[spots[0]].set(low).at[spots[1]].set(largest)


def strengthened(values, stream_key, source, target, blocks, factor):
    def block_of(axis_at):
        return (jnp.arange(values.shape[axis_at]) // (values.shape[axis_at] // blocks)).reshape((-1,) + (1,) * (values.ndim - 1 - axis_at))

    near = jax.random.permutation(stream_key, blocks)[block_of(target)]
    other_side = (block_of(target) + blocks // 2) % blocks
    return jnp.where((block_of(source) == near) | (block_of(source) == other_side), factor * values, values)


def steps_of(own_key, extent, shards, least, largest):
    level, own = 1.0, jax.random.fold_in(own_key, 6)
    for dim, blocks in shards:
        draws = jnp.exp(jax.random.uniform(jax.random.fold_in(own, dim), (blocks,), jnp.float32, least / len(shards), largest / len(shards)))
        level = level * jnp.repeat(draws, extent[dim] // blocks).reshape([-1 if axis == dim else 1 for axis in range(len(extent))])
    return level


def rank_table(count, skew):
    weights = [(1 << 20) // math.isqrt(standing ** skew) + 1 for standing in range(1, count + 1)]
    width = 1 + sum(weights) // (1 << 30)
    return np.cumsum(np.array([max(1, weight // width) for weight in weights]))


def ranked_ids(rng, extent, amount, skew):
    listing = rank_table(amount, skew)
    ticket = jax.random.randint(jax.random.fold_in(rng, 1), extent, 0, int(listing[amount - 1]))
    rank = jnp.searchsorted(jnp.asarray(listing, jnp.int32), ticket, side="right")
    return jax.random.permutation(jax.random.fold_in(rng, 2), amount)[rank].astype(jnp.int32)


def profile(number_of, total, most, lean):
    portions = [(1 << 20) // math.isqrt(grade ** lean) + 1 for grade in range(2, number_of + 1)]
    rest, given = total - most - (number_of - 1), [1] * (number_of - 1)
    while rest > 0:
        candidates = [i for i in range(number_of - 1) if given[i] < most]
        pool, budget = sum([portions[i] for i in candidates]), rest
        for i in candidates:
            more = min(most - given[i], max(1, budget * portions[i] // pool), rest)
            given[i] = given[i] + more
            rest = rest - more
    return np.array([most] + given)


def ragged(rng, number_of, total, most, lean):
    if number_of == 2:
        one = jax.random.randint(rng, (), max(1, total - most), min(most, total - 1) + 1)
        return jnp.stack([one, total - one])
    tallies = jnp.asarray(profile(number_of, total, most, lean), jnp.int32)
    couples = (number_of - 1) // 2
    source_of, receiver = tallies[1:1 + 2 * couples:2], tallies[2:2 + 2 * couples:2]
    room = jnp.minimum(source_of - 1, most - receiver)
    passed = jax.random.randint(jax.random.fold_in(rng, 1), (couples,), 0, 1 << 20) % (room + 1)
    tallies = tallies.at[1:1 + 2 * couples:2].set(source_of - passed).at[2:2 + 2 * couples:2].set(receiver + passed)
    return tallies[jax.random.permutation(jax.random.fold_in(rng, 2), number_of)]


def gaussian(stream_key, dims, scale, limit, cuts=(), kind=jnp.bfloat16):
    level = steps_of(stream_key, dims, cuts, -0.22, 0.18) if cuts else 1.0
    values = jax.random.normal(stream_key, dims, jnp.float32) * scale * level
    return jnp.minimum(jnp.maximum(values, -limit), limit).astype(kind)


def bell_draw_with(key, dims, scale, limit, pieces, heavy, kind=jnp.bfloat16):
    entries = scale * jax.random.normal(key, dims, jnp.float32)
    if pieces:
        entries = entries * steps_of(key, dims, pieces, -0.22, 0.18)
    return jnp.clip(strengthened(entries, jax.random.fold_in(key, 3), *heavy), -limit, limit).astype(kind)


def setup_inputs(seed: int = 0) -> dict:
    keys = jax.random.split(jax.random.key(seed), 14)
    return {
        "hidden_in": gaussian(keys[0], (2, TOKENS, D), 1.0, 6.0, ((1, 8), (2, 32))),
        "norm_gains": jnp.clip(1.0 + 0.15 * jax.random.normal(keys[1], (2, 2, D), jnp.float32), 0.25, 1.75),
        "w_qk": gaussian(keys[2], (2, D, 2 * HEADS * FEAT_IN), D ** -0.5, 0.125, ((1, 32),)),
        "w_v": gaussian(keys[3], (2, D, D), D ** -0.5, 0.125, ((2, 32),)),
        "w_o": bell_draw_with(keys[4], (2, D, D), D ** -0.5, 0.25, ((1, 32),), (1, 2, 32, 2.75)),
        "lm_head": draw_lm_head(jax.random.fold_in(keys[13], 71), 0),
        "state_pool": draw_state_pool(jax.random.fold_in(keys[13], 71), 0),
        "norm_pool": draw_norm_pool(jax.random.fold_in(keys[13], 71), 0),
        "seq_lens": jax.vmap(lambda own: ragged(own, SEQ_DEV, TOK_DEV, MOST_LEN, 2))(jax.random.split(keys[8], N_TOK)).reshape((N_TOK, SEQ_DEV)).astype(jnp.int32),
        "page_slot": draw_page_slot(jax.random.fold_in(keys[13], 71), 0),
        "fresh": plant((jax.random.randint(keys[10], (N_TOK, SEQ_DEV), 0, 4) < 1).astype(jnp.int32), jax.random.fold_in(keys[10], 1), 0, 1),
        "targets": plant(ranked_ids(keys[11], (TOKENS,), VOCAB, 2), jax.random.fold_in(keys[11], 3), 0, VOCAB - 1).astype(jnp.int32),
        "owner_slot": jax.random.permutation(keys[12], SEQS).astype(jnp.int32),
    }


EPSILON = 1e-05

def widen(array):
    return lax.optimization_barrier(array).astype(jnp.float32)

def taylor_feats(vector):
    lead = vector.shape[:-1]
    inner = vector.shape[-1]
    outer = vector[..., :, None] * vector[..., None, :]
    ones = jnp.ones_like(vector[..., :1])
    return jnp.concatenate([ones, vector, outer.reshape(lead + (inner * inner,)) * 0.5 ** 0.5], axis=-1)

def rms_norm(hidden, gain):
    widened = hidden.astype(jnp.float32)
    row_scale = lax.rsqrt(lax.optimization_barrier(jnp.mean(widened * widened, axis=-1, keepdims=True)) + EPSILON)
    return (widened * row_scale * gain).astype(jnp.bfloat16)

def score_group(hidden, seq_lengths, pool_rows, fresh_flags, target_ids, state_block, norm_block, norm_gains, w_qk, w_v, w_o, lm_head):
    tok_rows = hidden.shape[1]
    head_width = D // HEADS
    highest = lax.Precision.HIGHEST
    normed = rms_norm(hidden, norm_gains[:, 0][:, None, :])
    normed_wide = widen(normed)
    proj = jnp.einsum('mtd,mdc->mtc', normed_wide, w_qk.astype(jnp.float32))
    proj = proj.reshape(2, tok_rows, 2, HEADS, FEAT_IN) * FEAT_IN ** (-0.25)
    queries = proj[:, :, 0]
    keys_in = proj[:, :, 1]
    values_all = jnp.einsum('mtd,mdc->mtc', normed_wide, w_v.astype(jnp.float32)).astype(jnp.bfloat16)
    values_all = widen(values_all).reshape(2, tok_rows, HEADS, head_width)
    seq_ends = jnp.cumsum(seq_lengths).astype(jnp.int32)
    seq_starts = seq_ends - seq_lengths
    position = jnp.arange(tok_rows, dtype=jnp.int32)
    member = ((position[:, None] >= seq_starts[None, :]) & (position[:, None] < seq_ends[None, :])).astype(jnp.float32)
    seq_index = lax.optimization_barrier(jnp.sum((position[:, None] >= seq_ends[None, :]).astype(jnp.int32), axis=1))
    causal = (seq_index[:, None] == seq_index[None, :]) & (position[:, None] >= position[None, :])
    scores = jnp.einsum('mthf,muhf->mhtu', queries, keys_in, precision=highest)
    weights_f = jnp.where(causal[None, None], 1.0 + scores + 0.5 * scores * scores, 0.0)
    intra_den = lax.optimization_barrier(jnp.sum(weights_f, axis=-1))
    weights_b = widen(weights_f.astype(jnp.bfloat16))
    intra_num = jnp.einsum('mhtu,muhc->mthc', weights_b, values_all)
    kept = 1.0 - fresh_flags.astype(jnp.float32)
    prefix_states = state_block[pool_rows] * kept[:, None, None, None]
    prefix_states = prefix_states.reshape(SEQ_DEV, 2, FEAT, HEADS, head_width)
    prefix_norms = norm_block[pool_rows] * kept[:, None, None, None]
    query_feats = taylor_feats(queries)
    per_seq = jnp.einsum('mthf,smfhc->mtshc', query_feats, prefix_states, precision=highest)
    prefix_num = jnp.einsum('mtshc,ts->mthc', per_seq, member, precision=highest)
    per_seq_den = jnp.einsum('mthf,smhf->mtsh', query_feats, prefix_norms, precision=highest)
    prefix_den = jnp.einsum('mtsh,ts->mth', per_seq_den, member, precision=highest)
    denom = prefix_den + intra_den.transpose(0, 2, 1)
    mixed = ((prefix_num + intra_num) / denom[..., None]).astype(jnp.bfloat16).reshape(2, tok_rows, D)
    attn_out = jnp.einsum('mtc,mcd->mtd', widen(mixed), w_o.astype(jnp.float32))
    resid = (hidden.astype(jnp.float32) + attn_out).astype(jnp.bfloat16)
    final = rms_norm(resid, norm_gains[:, 1][:, None, :])
    logits = jnp.einsum('mtd,mvd->mtv', widen(final), lm_head.astype(jnp.float32))
    vocab_top = lax.optimization_barrier(jnp.max(logits, axis=-1))
    exp_total = lax.optimization_barrier(jnp.sum(jnp.exp(logits - vocab_top[..., None]), axis=-1))
    matches = jnp.arange(VOCAB, dtype=jnp.int32)[None, None, :] == target_ids[None, :, None]
    target_logit = lax.optimization_barrier(jnp.sum(jnp.where(matches, logits, 0.0), axis=-1))
    log_probs = target_logit - vocab_top - jnp.log(exp_total)
    seq_mean = jnp.dot(member.T, log_probs[0] - log_probs[1], precision=highest) / seq_lengths.astype(jnp.float32)
    return (log_probs, seq_mean)

def reference(hidden_in, norm_gains, w_qk, w_v, w_o, lm_head, state_pool, norm_pool, seq_lens, page_slot, fresh, targets, owner_slot):
    groups = (hidden_in.reshape(2, N_TOK, TOK_DEV, D).transpose(1, 0, 2, 3), seq_lens, page_slot, fresh, targets.reshape(N_TOK, TOK_DEV), state_pool.reshape(N_TOK, POOL, 2, FEAT, D), norm_pool.reshape(N_TOK, POOL, 2, HEADS, FEAT))

    def per_group(group):
        return score_group(*group, norm_gains, w_qk, w_v, w_o, lm_head)
    log_probs, seq_mean = lax.map(per_group, groups)
    token_logp = log_probs.transpose(1, 0, 2).reshape(2, TOKENS)
    seq_diffs = jnp.zeros((SEQS,), jnp.float32).at[owner_slot].set(seq_mean.reshape(SEQS))
    return (token_logp, seq_diffs)
```

```python
import functools

import jax
import jax.numpy as jnp
import numpy as np
from jax import lax
from jax.experimental import pallas as pl
from jax.experimental.pallas import tpu as pltpu
from jax.sharding import Mesh, PartitionSpec as P

HEADS = 16
FEAT_IN = 16
FEAT = 1 + FEAT_IN + FEAT_IN * FEAT_IN
EPSILON = 1e-05
RING = 4
CHIPS = RING * RING
SHIFTS = (0, 1, 3, 2)
BACK = (0, 2, 1, 3)
CHIP_AXES = ("x", "y")
BLK_AXES = ("x", "y", "core")
PAIR_ROWS = 9 * FEAT_IN
FOLDED = PAIR_ROWS + FEAT_IN + 16
HEAD_ROWS = 128
BF = jnp.bfloat16
F32 = jnp.float32


def fold_matrix():
    fold = np.zeros((FOLDED, FEAT), np.float32)
    root = np.float32(0.5**0.5)
    for step in range(9):
        for i in range(FEAT_IN):
            j = (i + step) % FEAT_IN
            row = step * FEAT_IN + i
            if step == 0:
                fold[row, 1 + FEAT_IN + i * FEAT_IN + i] = root
            else:
                share = root * np.float32(0.5 if step == 8 else 1.0)
                fold[row, 1 + FEAT_IN + i * FEAT_IN + j] = share
                fold[row, 1 + FEAT_IN + j * FEAT_IN + i] = share
    for i in range(FEAT_IN):
        fold[PAIR_ROWS + i, 1 + i] = 1.0
    fold[PAIR_ROWS + FEAT_IN, 0] = 1.0
    return fold


def contract_first(left, right):
    return lax.dot_general(left, right, (((0,), (0,)), ((), ())), preferred_element_type=F32)


def mm(left, right):
    return jnp.dot(left, right, preferred_element_type=F32)


def split(value):
    high = value.astype(BF)
    return high, (value - high.astype(F32)).astype(BF)


def whole_call(body, out_shape, scratch, flops, moved, scalars):
    return pl.pallas_call(
        body,
        out_shape=out_shape,
        grid_spec=pltpu.PrefetchScalarGridSpec(
            num_scalar_prefetch=1,
            grid=(1,),
            in_specs=[pl.BlockSpec(s, lambda i, sc, n=len(s): (0,) * n) for s in scalars],
            out_specs=[pl.BlockSpec(o.shape, lambda i, sc, n=len(o.shape): (0,) * n) for o in out_shape],
            scratch_shapes=scratch,
        ),
        cost_estimate=pl.CostEstimate(flops=flops, bytes_accessed=moved, transcendentals=0),
        compiler_params=pltpu.CompilerParams(dimension_semantics=("arbitrary",)),
    )


def project_body(place, gains, h0, h1, h2, h3, p0, p1, p2, p3, k0, k1, k2, k3, o0, o1, o2, o3, normed, qk_all):
    rows, tokens = h0.shape
    squares = jnp.zeros((1, tokens), F32)
    qk = jnp.zeros((4 * 32, tokens), F32)
    for j, (hid, key) in enumerate(zip((h0, h1, h2, h3), (k0, k1, k2, k3))):
        wide = hid[...].astype(F32)
        squares = squares + jnp.sum(wide * wide, axis=0, keepdims=True)
        at = pl.multiple_of(place[j] * rows, 16)
        scaled = (wide * gains[pl.ds(at, rows), :]).astype(BF)
        normed[pl.ds(at, rows), :] = scaled
        qk = qk + mm(key[...], scaled)
    for d in range(4):
        qk_all[d] = qk[d * 32 : (d + 1) * 32]
    high, low = split(squares)
    row = lax.broadcasted_iota(jnp.int32, (16, tokens), 0)
    tail = jnp.where(row == 0, high.astype(F32), jnp.where(row == 1, low.astype(F32), 0.0)).astype(BF)
    pieces = (p0, p1, p2, p3)
    for d, out in enumerate((o0, o1, o2, o3)):
        out[64 : 64 + rows, :] = mm(pieces[BACK[d]][:rows, :], normed[...]).astype(BF)
        mine_high, mine_low = split(qk_all[place[4 + d]])
        out[0:32, :] = mine_high
        out[32:64, :] = mine_low
        out[64 + rows :, :] = tail


def attend_body(ends, a0, a1, a2, a3, s_high, s_low, out):
    width = out.shape[0]
    tokens = out.shape[1]
    total = (
        a0[...].astype(F32) + a1[...].astype(F32) + a2[...].astype(F32) + a3[...].astype(F32)
    )
    model_width = width * CHIPS
    squares = total[64 + width : 65 + width] + total[65 + width : 66 + width]
    scale = lax.rsqrt(squares / model_width + EPSILON)
    qk = (total[0:32] + total[32:64]) * (scale * FEAT_IN ** (-0.25))
    query, key = qk[:FEAT_IN], qk[FEAT_IN:]
    values = (total[64 : 64 + width] * scale).astype(BF)
    where_t = lax.broadcasted_iota(jnp.int32, (1, tokens), 1)
    seq = jnp.zeros((1, tokens), jnp.int32)
    start = jnp.zeros((1, tokens), jnp.int32)
    seqs = ends.shape[0]
    for s in range(seqs):
        past = where_t >= ends[s]
        seq = seq + past.astype(jnp.int32)
        start = jnp.where(past, ends[s], start)
    doubled = jnp.concatenate([query, query], axis=0)
    rows = [query * doubled[d : d + FEAT_IN] for d in range(9)]
    one = jnp.where(lax.broadcasted_iota(jnp.int32, (16, tokens), 0) == 0, 1.0, 0.0)
    feats = jnp.concatenate(rows + [query, one], axis=0)
    f_high, f_low = split(feats)
    prefix = jnp.zeros((HEAD_ROWS, tokens), F32)
    for s in range(seqs):
        part_high = s_high[s * HEAD_ROWS : (s + 1) * HEAD_ROWS, :]
        part_low = s_low[s * HEAD_ROWS : (s + 1) * HEAD_ROWS, :]
        term = mm(part_high, f_high) + (mm(part_high, f_low) + mm(part_low, f_high))
        prefix = jnp.where(seq == s, term, prefix)
    q_high, q_low = split(query)
    k_high, k_low = split(key)
    q_cat = jnp.concatenate([q_high, q_low, q_high], axis=0)
    k_cat = jnp.concatenate([k_high, k_high, k_low], axis=0)
    step = 256
    for b in range(tokens // step):
        upto = (b + 1) * step
        cols = slice(b * step, upto)
        scores = contract_first(k_cat[:, :upto], q_cat[:, cols])
        where_u = lax.broadcasted_iota(jnp.int32, (upto, step), 0)
        seen = (where_u >= start[:, cols]) & (where_u <= where_t[:, cols])
        weights = jnp.where(seen, 1.0 + scores + 0.5 * scores * scores, 0.0)
        denom = prefix[width : width + 1, cols] + jnp.sum(weights, axis=0, keepdims=True)
        numer = prefix[:width, cols] + mm(values[:, :upto], weights.astype(BF))
        out[:, cols] = (numer / denom).astype(BF)


def output_body(place, m0, m1, m2, m3, p0, p1, p2, p3, o0, o1, o2, o3, acc):
    rows = m0.shape[0]
    total = jnp.zeros(acc.shape, F32)
    for mixed, piece in zip((m0, m1, m2, m3), (p0, p1, p2, p3)):
        total = total + contract_first(piece[rows:, :], mixed[...])
    acc[...] = total
    for d, out in enumerate((o0, o1, o2, o3)):
        at = pl.multiple_of(place[d] * rows, 16)
        out[...] = acc[pl.ds(at, rows), :].astype(out.dtype)


def logits_body(place, gains, targets, g0, g1, g2, g3, own, other, out, final, scale, top, total, hit):
    step = pl.program_id(0)
    tokens = final.shape[1]
    rows = final.shape[0] // CHIPS

    @pl.when(step == 0)
    def _():
        squares = jnp.zeros((1, tokens), F32)
        for p, group in enumerate((g0, g1, g2, g3)):
            for j in range(RING):
                wide = group[j * rows : (j + 1) * rows, :].astype(F32)
                squares = squares + jnp.sum(wide * wide, axis=0, keepdims=True)
                at = pl.multiple_of(place[p * RING + j] * rows, 16)
                final[pl.ds(at, rows), :] = (wide * gains[pl.ds(at, rows), :]).astype(BF)
        scale[...] = lax.rsqrt(squares / final.shape[0] + EPSILON)
        top[...] = jnp.full(top.shape, -jnp.inf, F32)
        total[...] = jnp.zeros(total.shape, F32)
        hit[...] = jnp.zeros(hit.shape, F32)

    count = other.shape[0]
    for part, base in ((own[0], place[CHIPS + 1]), (other[...], place[CHIPS + 2])):
        logits = mm(part, final[...]) * scale[...]
        ids = lax.broadcasted_iota(jnp.int32, (count, tokens), 0) + (base + step * count)
        found = jnp.where(ids == targets[...], logits, 0.0)
        hit[...] += jnp.sum(found.reshape(count // 8, 8, tokens), axis=0)
        grouped = logits.reshape(count // 8, 8, tokens)
        before = top[...]
        after = jnp.maximum(before, jnp.max(grouped, axis=0))
        top[...] = after
        total[...] = total[...] * jnp.exp(before - after) + jnp.sum(
            jnp.exp(grouped - after[None]), axis=0
        )

    @pl.when(step == pl.num_programs(0) - 1)
    def _():
        best = jnp.max(top[...], axis=0, keepdims=True)
        mass = jnp.sum(total[...] * jnp.exp(top[...] - best), axis=0, keepdims=True)
        out[0:1, :] = best + jnp.log(mass)
        out[1:2, :] = jnp.sum(hit[...], axis=0, keepdims=True)


def score_vocab(place, gains, targets, groups, lm_head, other):
    rows, tokens = groups[0].shape
    model_width = rows * RING
    voc = lm_head.shape[1]
    block = 128
    full = lambda shape: pl.BlockSpec(shape, lambda i, sc: (0,) * len(shape))
    return pl.pallas_call(
        logits_body,
        out_shape=jax.ShapeDtypeStruct((2, tokens), F32),
        grid_spec=pltpu.PrefetchScalarGridSpec(
            num_scalar_prefetch=1,
            grid=(voc // block,),
            in_specs=[full((model_width, 1)), full((1, tokens))]
            + [full((rows, tokens))] * 4
            + [
                pl.BlockSpec((1, block, model_width), lambda i, sc: (sc[CHIPS], i, 0)),
                pl.BlockSpec((block, model_width), lambda i, sc: (i, 0)),
            ],
            out_specs=full((2, tokens)),
            scratch_shapes=[
                pltpu.VMEM((model_width, tokens), BF),
                pltpu.VMEM((1, tokens), F32),
                pltpu.VMEM((8, tokens), F32),
                pltpu.VMEM((8, tokens), F32),
                pltpu.VMEM((8, tokens), F32),
            ],
        ),
        cost_estimate=pl.CostEstimate(
            flops=4 * voc * model_width * tokens,
            bytes_accessed=4 * voc * model_width + 2 * model_width * tokens,
            transcendentals=2 * voc * tokens,
        ),
        compiler_params=pltpu.CompilerParams(dimension_semantics=("arbitrary",)),
    )(place, gains, targets, *groups, lm_head, other)


def send(value, axis, shift):
    count = lax.axis_size(axis)
    return lax.ppermute(value, axis, [(i, (i + shift) % count) for i in range(count)])


def spread(value, axis):
    return [value] + [send(value, axis, s) for s in SHIFTS[1:]]


def deal(table, where, axis):
    own = lax.dynamic_index_in_dim(table, where, 0, keepdims=False)
    parts = [
        send(lax.dynamic_index_in_dim(table, (where + s) % RING, 0, keepdims=False), axis, s)
        for s in SHIFTS[1:]
    ]
    return [own] + parts


def torus_pairs(shift, turn):
    pairs = []
    for x in range(RING):
        for y in range(RING):
            for core in range(2):
                along_x = (core == 0) != (turn == 1)
                to = ((x + shift) % RING, y) if along_x else (x, (y + shift) % RING)
                pairs.append(((x * RING + y) * 2 + core, (to[0] * RING + to[1]) * 2 + core))
    return pairs


def per_device(
    hidden_in,
    norm_gains,
    w_qk,
    w_v,
    w_o,
    lm_head,
    state_pool,
    norm_pool,
    seq_lens,
    page_slot,
    fresh,
    targets,
    owner_slot,
):
    highest = lax.Precision.HIGHEST
    x = lax.axis_index("x")
    y = lax.axis_index("y")
    core = lax.axis_index("core")
    chip = x * RING + y
    tokens = hidden_in.shape[1]
    half = hidden_in.shape[2]
    width = 2 * half
    quarter = RING * width
    model_width = CHIPS * width
    voc = lm_head.shape[1]
    shifts = jnp.array(SHIFTS, jnp.int32)

    def mine(value):
        return lax.dynamic_index_in_dim(value, core, 0, keepdims=False)

    def joined(value, axis):
        own = mine(value)
        came = send(lax.dynamic_index_in_dim(value, 1 - core, 0, keepdims=False), "core", 1)
        first = jnp.where(core == 0, own, came)
        second = jnp.where(core == 0, came, own)
        return jnp.concatenate([first, second], axis=axis)

    hidden = joined(hidden_in.transpose(0, 2, 1), 0)
    hidden_parts = spread(hidden, "y")

    qk_rows = joined(w_qk.transpose(0, 2, 1), 1)
    qk_table = (
        qk_rows.reshape(2, RING, RING, FEAT_IN, width)
        .transpose(2, 1, 0, 3, 4)
        .reshape(RING, RING * 2 * FEAT_IN, width)
    )
    qk_parts = deal(qk_table, y, "y")

    both = jnp.stack([w_v.transpose(0, 2, 1), w_o], axis=1)
    both = joined(both, 1)
    both_table = (
        both.reshape(2 * width, RING, quarter).transpose(1, 0, 2)
    )
    both_parts = deal(both_table, x, "x")

    fold = jnp.asarray(fold_matrix())
    pool_rows = page_slot[0]
    seqs = pool_rows.shape[0]
    kept = 1.0 - fresh[0].astype(F32)
    states = jnp.take(state_pool, pool_rows, axis=0) * kept[:, None, None, None]
    states = jnp.einsum("smfc,gf->mscg", states, fold, precision=highest)
    states = joined(states, 1)
    norms = mine(jnp.take(norm_pool, pool_rows, axis=0).transpose(1, 0, 2, 3))
    norms = lax.dynamic_index_in_dim(norms, chip, 1, keepdims=False) * kept[:, None]
    norms = jnp.dot(norms, fold.T, precision=highest)
    states = jnp.concatenate(
        [states, norms[:, None], jnp.zeros((seqs, HEAD_ROWS - width - 1, FOLDED), F32)], axis=1
    ).reshape(seqs * HEAD_ROWS, FOLDED)
    s_high, s_low = split(states)

    other_head = send(lax.dynamic_index_in_dim(lm_head, 1 - core, 0, keepdims=False), "core", 1)

    gains = mine(norm_gains)
    gains_in = lax.dynamic_slice_in_dim(gains[0], x * quarter, quarter, 0)[:, None]
    place = jnp.concatenate([(y - shifts) % RING, (x + shifts) % RING])
    sent_rows = 64 + width + 16
    payload = jax.ShapeDtypeStruct((sent_rows, tokens), BF)
    projected = whole_call(
        project_body,
        [payload] * 4,
        [pltpu.VMEM((quarter, tokens), BF), pltpu.VMEM((RING, 32, tokens), F32)],
        2 * tokens * quarter * (width + 32) * 4,
        tokens * quarter * 2 + 8 * sent_rows * tokens,
        [(quarter, 1)] + [(width, tokens)] * 4 + [(2 * width, quarter)] * 4 + [(128, width)] * 4,
    )(place, gains_in, *hidden_parts, *both_parts, *qk_parts)
    summands = [projected[0]] + [
        send(part, "x", s) for part, s in zip(projected[1:], SHIFTS[1:])
    ]

    seq_lengths = seq_lens[0]
    seq_ends = jnp.cumsum(seq_lengths)
    seq_starts = seq_ends - seq_lengths
    (mixed,) = whole_call(
        attend_body,
        [jax.ShapeDtypeStruct((width, tokens), BF)],
        [],
        2 * tokens * tokens * (width + 48) + 6 * tokens * FOLDED * HEAD_ROWS * seqs,
        8 * sent_rows * tokens + 4 * seqs * HEAD_ROWS * FOLDED,
        [(sent_rows, tokens)] * 4 + [(seqs * HEAD_ROWS, FOLDED)] * 2,
    )(seq_ends, *summands, s_high, s_low)
    mixed_parts = spread(mixed, "x")

    place = (y + shifts) % RING
    shares = whole_call(
        output_body,
        [jax.ShapeDtypeStruct((width, tokens), F32)] + [jax.ShapeDtypeStruct((width, tokens), BF)] * 3,
        [pltpu.VMEM((quarter, tokens), F32)],
        2 * tokens * quarter * quarter,
        10 * tokens * quarter,
        [(width, tokens)] * 4 + [(2 * width, quarter)] * 4,
    )(place, *mixed_parts, *both_parts)
    total = hidden.astype(F32) + shares[0]
    for part, s in zip(shares[1:], SHIFTS[1:]):
        total = total + send(part, "y", s).astype(F32)
    resid = total.astype(BF)

    line = jnp.concatenate(
        [resid] + [lax.ppermute(resid, BLK_AXES, torus_pairs(s, 0)) for s in SHIFTS[1:]], axis=0
    )
    groups = [line] + [lax.ppermute(line, BLK_AXES, torus_pairs(s, 1)) for s in SHIFTS[1:]]
    first = shifts[None, :]
    second = shifts[:, None]
    from_x = jnp.where(core == 0, x - first, x - second) % RING
    from_y = jnp.where(core == 0, y - second, y - first) % RING
    place = jnp.concatenate(
        [
            (from_x * RING + from_y).reshape(-1),
            jnp.stack([core, (chip * 2 + core) * voc, (chip * 2 + 1 - core) * voc]),
        ]
    ).astype(jnp.int32)
    stats = score_vocab(place, gains[1][:, None], targets[None], groups, lm_head, other_head)

    table = lax.all_to_all(
        jnp.broadcast_to(stats[None], (2 * CHIPS,) + stats.shape), BLK_AXES, 0, 0, tiled=True
    ).reshape(CHIPS, 2, 2, tokens)
    local = table[:, :, 0]
    best = jnp.max(local, axis=0)
    log_sum = best + jnp.log(jnp.sum(jnp.exp(local - best), axis=0))
    log_probs = jnp.sum(table[:, :, 1], axis=0) - log_sum

    position = jnp.arange(tokens, dtype=jnp.int32)
    member = (
        (position[None, :] >= seq_starts[:, None]) & (position[None, :] < seq_ends[:, None])
    ).astype(F32)
    seq_mean = jnp.sum(member * (log_probs[0] - log_probs[1])[None], axis=1) / seq_lengths.astype(F32)
    table = lax.all_gather(jnp.stack([seq_mean, owner_slot.astype(F32)]), "tok", axis=0)
    slots = (lax.axis_index("tok") * seqs + jnp.arange(seqs, dtype=jnp.int32)).astype(F32)
    named = slots[:, None, None] == table[None, :, 1]
    seq_diffs = jnp.sum(jnp.where(named, table[None, :, 0], 0.0), axis=(1, 2))
    return (log_probs, seq_diffs)


def solution(mesh):
    fine = Mesh(
        mesh.devices.reshape(RING, RING, 2, mesh.shape["tok"]), ("x", "y", "core", "tok")
    )
    blk = BLK_AXES
    placed = (
        P(None, "tok", blk),
        P(),
        P(None, blk, None),
        P(None, None, blk),
        P(None, blk, None),
        P(None, blk, None),
        P("tok", None, None, blk),
        P("tok", None, None, None),
        P("tok", None),
        P("tok", None),
        P("tok", None),
        P("tok"),
        P("tok"),
    )
    return jax.shard_map(
        per_device,
        mesh=fine,
        in_specs=placed,
        out_specs=(P(None, "tok"), P("tok")),
        check_vma=False,
    )
```

```python
import jax
import jax.numpy as jnp
from jax import lax
from jax.experimental import pallas as pl
from jax.experimental.pallas import tpu as pltpu
from jax.sharding import Mesh, PartitionSpec as P

HEADS = 16
FEAT_IN = 16
EPSILON = 1e-05
RING = 4
CHIPS = RING * RING
SHIFTS = (0, 1, 3, 2)
BLK_AXES = ("x", "y", "core")
VOC_STEPS = 4
BF = jnp.bfloat16
F32 = jnp.float32


def contract_first(left, right):
    return lax.dot_general(left, right, (((0,), (0,)), ((), ())), preferred_element_type=F32)


def mm(left, right):
    return jnp.dot(left, right, preferred_element_type=F32)


def split(value):
    high = value.astype(BF)
    return high, (value - high.astype(F32)).astype(BF)


def whole(shape):
    return pl.BlockSpec(shape, lambda i, *scalars: (0,) * len(shape))


def place_groups(spot, groups, final):
    rows = final.shape[0] // CHIPS
    x, y, core = spot[0], spot[1], spot[2]
    squares = jnp.zeros((1, final.shape[1]), F32)
    for p, group in enumerate(groups):
        for j in range(RING):
            inner, outer = RING - SHIFTS[j], RING - SHIFTS[p]
            from_x = lax.rem(x + jnp.where(core == 0, inner, outer), RING)
            from_y = lax.rem(y + jnp.where(core == 0, outer, inner), RING)
            at = pl.multiple_of((from_x * RING + from_y) * rows, 16)
            wide = group[j * rows : (j + 1) * rows, :].astype(F32)
            squares = squares + jnp.sum(wide * wide, axis=0, keepdims=True)
            final[pl.ds(at, rows), :] = group[j * rows : (j + 1) * rows, :]
    return lax.rsqrt(squares / final.shape[0] + EPSILON)


def deal_body(w_o, w_qk, out_o, out_qk):
    quarter = out_o.shape[2]
    for m in range(2):
        for q in range(RING):
            out_o[q * 2 + m] = w_o[m, :, q * quarter : (q + 1) * quarter]
        columns = w_qk[m].astype(F32).T.astype(BF)
        for h in range(HEADS):
            for g in range(2):
                at = (g * HEADS + h) * FEAT_IN
                out_qk[h * 2 + m, g * FEAT_IN : (g + 1) * FEAT_IN, :] = columns[at : at + FEAT_IN]


def deal_weights(w_o, w_qk):
    _, half, model_width = w_o.shape
    outs = [
        jax.ShapeDtypeStruct((2 * RING, half, model_width // RING), BF),
        jax.ShapeDtypeStruct((2 * HEADS, 2 * FEAT_IN, half), BF),
    ]
    return pl.pallas_call(
        deal_body,
        out_shape=outs,
        grid=(1,),
        in_specs=[whole(w_o.shape), whole(w_qk.shape)],
        out_specs=[whole(out.shape) for out in outs],
        cost_estimate=pl.CostEstimate(flops=0, bytes_accessed=2 << 20, transcendentals=0),
    )(w_o, w_qk)


def mix_body(
    spot, lens, slots, fresh, norm_gains, g0, g1, g2, g3, v_own, v_came, w_qk, s_own, s_other, norms,
    out, hidden, columns,
):
    width, tokens = out.shape
    half = width // 2
    seqs = lens.shape[1]
    first_core = spot[2] == 0
    core = spot[2]
    scale = place_groups(spot, (g0, g1, g2, g3), hidden)
    gains = norm_gains[core][0:1, :]
    for source in range(2 * CHIPS):
        columns[:, source * half : (source + 1) * half] = w_qk[source].astype(F32)
    qk = mm((columns[...] * gains).astype(BF), hidden[...]) * (scale * FEAT_IN ** (-0.25))
    query, key = qk[:FEAT_IN], qk[FEAT_IN:]
    own = mm((v_own[0].astype(F32) * gains).astype(BF), hidden[...])
    other = mm((v_came[0].astype(F32) * gains).astype(BF), hidden[...])
    values = jnp.concatenate(
        [jnp.where(first_core, own, other), jnp.where(first_core, other, own)], axis=0
    )
    values = (values * scale).astype(BF)
    where_t = lax.broadcasted_iota(jnp.int32, (1, tokens), 1)
    seq = jnp.zeros((1, tokens), jnp.int32)
    start = jnp.zeros((1, tokens), jnp.int32)
    kept = jnp.full((1, tokens), 1 - fresh[0, 0], jnp.int32)
    end = lens[0, 0]
    for s in range(1, seqs):
        past = where_t >= end
        seq = jnp.where(past, s, seq)
        start = jnp.where(past, end, start)
        kept = jnp.where(past, 1 - fresh[0, s], kept)
        end = end + lens[0, s]
    kept = kept.astype(F32)
    pairs = [query[i : i + 1] * query * 0.5**0.5 for i in range(FEAT_IN)]
    feats = jnp.concatenate([jnp.ones((1, tokens), F32), query] + pairs, axis=0)
    f_high, f_low = split(feats)
    head = spot[0] * RING + spot[1]
    n_high, n_low = split(
        jnp.concatenate([norms[slots[0, s], 0, pl.ds(head, 1), :] for s in range(seqs)], axis=0)
    )
    dens = mm(n_high, f_high) + (mm(n_high, f_low) + mm(n_low, f_high))
    picked = lax.broadcasted_iota(jnp.int32, dens.shape, 0) == seq
    prefix_den = jnp.sum(jnp.where(picked, dens, 0.0), axis=0, keepdims=True) * kept
    near = jnp.zeros((half, tokens), F32)
    far = jnp.zeros((half, tokens), F32)
    for s in range(seqs):
        near = jnp.where(seq == s, mm(s_own[s], f_high), near)
        far = jnp.where(seq == s, mm(s_other[s], f_high), far)
    prefix = (
        jnp.concatenate([jnp.where(first_core, near, far), jnp.where(first_core, far, near)], axis=0)
        * kept
    )
    q_high, q_low = split(query)
    k_high, k_low = split(key)
    q_cat = jnp.concatenate([q_high, q_low, q_high], axis=0)
    k_cat = jnp.concatenate([k_high, k_high, k_low], axis=0)
    step = 256
    for b in range(tokens // step):
        upto = (b + 1) * step
        cols = slice(b * step, upto)
        scores = contract_first(k_cat[:, :upto], q_cat[:, cols])
        where_u = lax.broadcasted_iota(jnp.int32, (upto, step), 0)
        seen = (where_u >= start[:, cols]) & (where_u <= where_t[:, cols])
        weights = jnp.where(seen, 1.0 + scores + 0.5 * scores * scores, 0.0)
        denom = prefix_den[:, cols] + jnp.sum(weights, axis=0, keepdims=True)
        numer = prefix[:, cols] + mm(values[:, :upto], weights.astype(BF))
        out[:, cols] = (numer / denom).astype(BF)


def mix_heads(spot, lens, slots, fresh, norm_gains, groups, v_own, v_came, w_qk, s_own, s_other, norm_pool):
    rows, tokens = groups[0].shape
    model_width = rows * RING
    half = v_own.shape[1]
    pool, _, heads, feats = norm_pool.shape
    per_model = pl.BlockSpec((1, half, model_width), lambda i, spot, *scalars: (spot[2], 0, 0))
    return pl.pallas_call(
        mix_body,
        out_shape=jax.ShapeDtypeStruct((2 * half, tokens), BF),
        grid_spec=pltpu.PrefetchScalarGridSpec(
            num_scalar_prefetch=4,
            grid=(1,),
            in_specs=[whole(norm_gains.shape)]
            + [whole((rows, tokens))] * 4
            + [
                per_model,
                per_model,
                whole(w_qk.shape),
                whole(s_own.shape),
                whole(s_other.shape),
                pl.BlockSpec((pool, 1, heads, feats), lambda i, spot, *scalars: (0, spot[2], 0, 0)),
            ],
            out_specs=whole((2 * half, tokens)),
            scratch_shapes=[
                pltpu.VMEM((model_width, tokens), BF),
                pltpu.VMEM((2 * FEAT_IN, model_width), F32),
            ],
        ),
        cost_estimate=pl.CostEstimate(
            flops=2 * tokens * (model_width * 144 + tokens * 160 + 8 * 273 * 112),
            bytes_accessed=2 * model_width * (tokens + 144) + 4 * s_own.size,
            transcendentals=0,
        ),
        compiler_params=pltpu.CompilerParams(dimension_semantics=("arbitrary",)),
    )(spot, lens, slots, fresh, norm_gains, *groups, v_own, v_came, w_qk, s_own, s_other, norm_pool)


def output_body(spot, m0, m1, m2, m3, weights, o0, o1, o2, o3, mixed, acc):
    rows = m0.shape[0]
    for j, piece in enumerate((m0, m1, m2, m3)):
        at = pl.multiple_of(lax.rem(spot[0] + RING - SHIFTS[j], RING) * rows, 16)
        mixed[pl.ds(at, rows), :] = piece[...]
    acc[...] = contract_first(weights[...], mixed[...])
    for d, out in enumerate((o0, o1, o2, o3)):
        at = pl.multiple_of(lax.rem(spot[1] + SHIFTS[d], RING) * rows, 16)
        out[...] = acc[pl.ds(at, rows), :].astype(out.dtype)


def output_shares(spot, parts, weights):
    rows, tokens = parts[0].shape
    quarter = RING * rows
    outs = [jax.ShapeDtypeStruct((rows, tokens), F32)] + [jax.ShapeDtypeStruct((rows, tokens), BF)] * 3
    return pl.pallas_call(
        output_body,
        out_shape=outs,
        grid_spec=pltpu.PrefetchScalarGridSpec(
            num_scalar_prefetch=1,
            grid=(1,),
            in_specs=[whole((rows, tokens))] * 4 + [whole((quarter, quarter))],
            out_specs=[whole((rows, tokens))] * 4,
            scratch_shapes=[pltpu.VMEM((quarter, tokens), BF), pltpu.VMEM((quarter, tokens), F32)],
        ),
        cost_estimate=pl.CostEstimate(
            flops=2 * tokens * quarter * quarter,
            bytes_accessed=2 * quarter * quarter + 5 * quarter * tokens,
            transcendentals=0,
        ),
        compiler_params=pltpu.CompilerParams(
            dimension_semantics=("arbitrary",), vmem_limit_bytes=12 << 20
        ),
    )(spot, *parts, weights)


def scale_body(spot, norm_gains, own, came, out):
    gains = norm_gains[spot[2]][1:2, :]
    for part, rows in enumerate((own, came)):
        out[part] = (rows[0].astype(F32) * gains).astype(BF)


def scale_heads(spot, norm_gains, lm_head, came_head):
    _, voc, model_width = lm_head.shape
    block = voc // 7
    rows = pl.BlockSpec((1, block, model_width), lambda i, spot: (spot[2], i, 0))
    return pl.pallas_call(
        scale_body,
        out_shape=jax.ShapeDtypeStruct((2, voc, model_width), BF),
        grid_spec=pltpu.PrefetchScalarGridSpec(
            num_scalar_prefetch=1,
            grid=(7,),
            in_specs=[whole(norm_gains.shape), rows, rows],
            out_specs=pl.BlockSpec((2, block, model_width), lambda i, spot: (0, i, 0)),
        ),
        cost_estimate=pl.CostEstimate(
            flops=2 * voc * model_width, bytes_accessed=8 * voc * model_width, transcendentals=0
        ),
        compiler_params=pltpu.CompilerParams(
            dimension_semantics=("arbitrary",), vmem_limit_bytes=8 << 20
        ),
    )(spot, norm_gains, lm_head, came_head)


def logits_body(
    spot, targets, g0, g1, g2, g3, heads, prior, out, final, scale, top, total, hit
):
    step = pl.program_id(0)
    tokens = final.shape[1]
    core = spot[2]

    @pl.when(step == 0)
    def _():
        scale[...] = place_groups(spot, (g0, g1, g2, g3), final)
        top[...] = jnp.full(top.shape, -jnp.inf, F32)
        total[...] = jnp.zeros(total.shape, F32)
        hit[...] = jnp.zeros(hit.shape, F32)

    count = heads.shape[1] // VOC_STEPS
    device = (spot[0] * RING + spot[1]) * 2
    at = pl.multiple_of(step * count, 16)
    for part, holder in ((0, core), (1, 1 - core)):
        logits = mm(heads[part, pl.ds(at, count), :], final[...]) * scale[...]
        base = ((device + holder) * pl.num_programs(0) + step) * count
        ids = lax.broadcasted_iota(jnp.int32, (count, tokens), 0)
        found = jnp.where(ids == targets[...] - base, logits, 0.0)
        hit[...] += jnp.sum(found.reshape(count // 8, 8, tokens), axis=0)
        grouped = logits.reshape(count // 8, 8, tokens)
        before = top[...]
        after = jnp.maximum(before, jnp.max(grouped, axis=0))
        top[...] = after
        total[...] = total[...] * jnp.exp(before - after) + jnp.sum(
            jnp.exp(grouped - after[None]), axis=0
        )

    @pl.when(step == pl.num_programs(0) - 1)
    def _():
        best = jnp.max(top[...], axis=0, keepdims=True)
        mass = jnp.sum(total[...] * jnp.exp(top[...] - best), axis=0, keepdims=True)
        found = jnp.sum(hit[...], axis=0, keepdims=True)
        pair = jnp.concatenate([best + jnp.log(mass), found], axis=0)
        if prior is not None:
            pair = jnp.concatenate([prior[...], pair], axis=1)
        out[...] = jnp.broadcast_to(pair, out.shape)


def score_vocab(spot, targets, groups, heads, prior):
    rows, tokens = groups[0].shape
    model_width = rows * RING
    voc = heads.shape[1]
    if prior is None:
        body = lambda *refs: logits_body(*refs[:7], None, *refs[7:])
        out = jax.ShapeDtypeStruct((2, tokens), F32)
    else:
        body = logits_body
        out = jax.ShapeDtypeStruct((2 * CHIPS, 2, prior.shape[1] + tokens), F32)
    return pl.pallas_call(
        body,
        out_shape=out,
        grid_spec=pltpu.PrefetchScalarGridSpec(
            num_scalar_prefetch=1,
            grid=(VOC_STEPS,),
            in_specs=[whole((1, tokens))]
            + [whole((rows, tokens))] * 4
            + [pl.BlockSpec(memory_space=pltpu.VMEM)]
            + ([] if prior is None else [whole(prior.shape)]),
            out_specs=whole(out.shape),
            scratch_shapes=[
                pltpu.VMEM((model_width, tokens), BF),
                pltpu.VMEM((1, tokens), F32),
                pltpu.VMEM((8, tokens), F32),
                pltpu.VMEM((8, tokens), F32),
                pltpu.VMEM((8, tokens), F32),
            ],
        ),
        cost_estimate=pl.CostEstimate(
            flops=4 * voc * model_width * tokens,
            bytes_accessed=4 * voc * model_width + 2 * model_width * tokens,
            transcendentals=2 * voc * tokens,
        ),
        compiler_params=pltpu.CompilerParams(
            dimension_semantics=("arbitrary",), vmem_limit_bytes=24 << 20
        ),
    )(spot, targets, *groups, heads, *([] if prior is None else [prior]))


def join_body(p0, p1, p2, p3, *outs):
    rows = p0.shape[0]
    at = 0
    for out in outs:
        width = out.shape[1]
        for j, piece in enumerate((p0, p1, p2, p3)):
            out[j * rows : (j + 1) * rows, :] = piece[:, at : at + width]
        at += width


def join(pieces, widths, limit):
    rows, tokens = pieces[0].shape
    outs = [jax.ShapeDtypeStruct((RING * rows, width), BF) for width in widths]
    return pl.pallas_call(
        join_body,
        out_shape=outs,
        grid=(1,),
        in_specs=[whole((rows, tokens))] * RING,
        out_specs=[whole(out.shape) for out in outs],
        cost_estimate=pl.CostEstimate(
            flops=0, bytes_accessed=4 * RING * rows * tokens, transcendentals=0
        ),
        compiler_params=pltpu.CompilerParams(
            dimension_semantics=("arbitrary",), vmem_limit_bytes=limit
        ),
    )(*pieces)


def send(value, axis, shift):
    count = lax.axis_size(axis)
    return lax.ppermute(value, axis, [(i, (i + shift) % count) for i in range(count)])


def spread(value, axis):
    return [value] + [send(value, axis, s) for s in SHIFTS[1:]]


def torus_pairs(shift, turn):
    pairs = []
    for x in range(RING):
        for y in range(RING):
            for core in range(2):
                along_x = (core == 0) != (turn == 1)
                to = ((x + shift) % RING, y) if along_x else (x, (y + shift) % RING)
                pairs.append(((x * RING + y) * 2 + core, (to[0] * RING + to[1]) * 2 + core))
    return pairs


def gather_line(value):
    parts = [lax.ppermute(value, BLK_AXES, torus_pairs(s, 0)) for s in SHIFTS[1:]]
    return [value] + parts


def gather_groups(line):
    return [line] + [lax.ppermute(line, BLK_AXES, torus_pairs(s, 1)) for s in SHIFTS[1:]]


def per_device(
    hidden_in,
    norm_gains,
    w_qk,
    w_v,
    w_o,
    lm_head,
    state_pool,
    norm_pool,
    seq_lens,
    page_slot,
    fresh,
    targets,
    owner_slot,
):
    x = lax.axis_index("x")
    y = lax.axis_index("y")
    core = lax.axis_index("core")
    chip = x * RING + y
    spot = jnp.stack([x, y, core]).astype(jnp.int32)
    tokens = hidden_in.shape[1]
    half = hidden_in.shape[2]
    width = 2 * half
    quarter = RING * width

    def mine(value):
        return lax.dynamic_index_in_dim(value, core, 0, keepdims=False)

    def theirs(value):
        return lax.dynamic_index_in_dim(value, 1 - core, 0, keepdims=False)

    def swap(value):
        return send(value, "core", 1)

    hidden_rows = hidden_in.transpose(0, 2, 1)
    came = mine(swap(hidden_rows))
    own = mine(hidden_rows)
    hidden = jnp.concatenate(
        [jnp.where(core == 0, own, came), jnp.where(core == 0, came, own)], axis=0
    )
    pieces = gather_line(hidden)
    out_sent, qk_sent = deal_weights(w_o, w_qk)
    out_here = lax.all_to_all(out_sent, ("x", "core"), 0, 0, tiled=True).reshape(quarter, quarter)
    states = jnp.take(state_pool.transpose(1, 0, 3, 2), page_slot[0], axis=1, mode="clip").astype(BF)
    s_other = swap(theirs(states))
    s_own = mine(states)
    pieces[3], out_here, s_other = lax.optimization_barrier((pieces[3], out_here, s_other))
    (line,) = join(pieces, [tokens], None)
    groups = gather_groups(line)

    v_rows = w_v.transpose(0, 2, 1)
    v_came = swap(v_rows)
    came_head = swap(lm_head)
    qk_sent, _ = lax.optimization_barrier((qk_sent, line))
    qk_here = lax.all_to_all(qk_sent, BLK_AXES, 0, 0, tiled=True)

    mixed = mix_heads(
        spot, seq_lens, page_slot, fresh, norm_gains, groups, v_rows, v_came, qk_here,
        s_own, s_other, norm_pool,
    )
    shares = output_shares(spot, spread(mixed, "x"), out_here)
    total = hidden.astype(F32) + shares[0]
    for part, s in zip(shares[1:], SHIFTS[1:]):
        total = total + send(part, "y", s).astype(F32)
    resid = total.astype(BF)

    pieces = gather_line(resid)
    stats = None
    cuts = ((0, 2 * tokens // 3), (2 * tokens // 3, tokens))
    lines = join(pieces, [end - at for at, end in cuts], 8 << 20)
    gathered = [gather_groups(line) for line in lines]
    late_gains, _ = lax.optimization_barrier((norm_gains, lines[0]))
    sources = [pltpu.with_memory_space_constraint(head, pltpu.HBM) for head in (lm_head, came_head)]
    heads = scale_heads(spot, late_gains, *sources)
    heads = pltpu.with_memory_space_constraint(heads, pltpu.VMEM)
    for (at, end), groups in zip(cuts, gathered):
        stats = score_vocab(
            spot, targets[None, at:end], groups, heads, stats
        )

    table = lax.all_to_all(stats, BLK_AXES, 0, 0, tiled=True).reshape(CHIPS, 2, 2, tokens)
    local = table[:, :, 0]
    best = jnp.max(local, axis=0)
    log_sum = best + jnp.log(jnp.sum(jnp.exp(local - best), axis=0))
    log_probs = jnp.sum(table[:, :, 1], axis=0) - log_sum

    seq_lengths = seq_lens[0]
    seqs = seq_lengths.shape[0]
    seq_ends = jnp.cumsum(seq_lengths)
    seq_starts = seq_ends - seq_lengths
    position = jnp.arange(tokens, dtype=jnp.int32)
    member = (
        (position[None, :] >= seq_starts[:, None]) & (position[None, :] < seq_ends[:, None])
    ).astype(F32)
    seq_mean = jnp.sum(member * (log_probs[0] - log_probs[1])[None], axis=1) / seq_lengths.astype(F32)
    count = lax.axis_size("tok")
    mean = jnp.stack([seq_mean, owner_slot.astype(F32)])
    near = jnp.stack([mean, send(mean, "tok", 1), send(mean, "tok", count - 1)])
    table = jnp.concatenate([near, send(near, "tok", 3), send(near, "tok", count - 3)[:2]], axis=0)
    slots = (lax.axis_index("tok") * seqs + jnp.arange(seqs, dtype=jnp.int32)).astype(F32)
    named = slots[:, None, None] == table[None, :, 1]
    seq_diffs = jnp.sum(jnp.where(named, table[None, :, 0], 0.0), axis=(1, 2))
    return (log_probs, seq_diffs)


def solution(mesh):
    fine = Mesh(
        mesh.devices.reshape(RING, RING, 2, mesh.shape["tok"]), ("x", "y", "core", "tok")
    )
    blk = BLK_AXES
    placed = (
        P(None, "tok", blk),
        P(),
        P(None, blk, None),
        P(None, None, blk),
        P(None, blk, None),
        P(None, blk, None),
        P("tok", None, None, blk),
        P("tok", None, None, None),
        P("tok", None),
        P("tok", None),
        P("tok", None),
        P("tok"),
        P("tok"),
    )
    return jax.shard_map(
        per_device,
        mesh=fine,
        in_specs=placed,
        out_specs=(P(None, "tok"), P("tok")),
        check_vma=False,
    )
```
